256 devices in a mesh: row: 32 (over z, y_lo, core), col: 8 (over y_hi, x).
Axes of the slice: x: 4, y: 4 (y_hi: 2, y_lo: 2; y = y_hi * 2 + y_lo), z: 8, core: 2. Of those that a mesh axis runs over, the one named last changes fastest.
Arguments:
- coupling: bfloat16 [16384, 4096], P('row', 'col'), may hold values from 0.19921875 to 5
- source_dist: bfloat16 [16384, 16384], P('row'), may hold values from -0.013531647 to 0.013531647, as said below
- target_dist: bfloat16 [4096, 4096], P('row', 'col'), may hold values from -0.09375 to 0.09375
- source_feat: bfloat16 [16384, 256], P('row'), may hold values from -3.5 to 3.5
- target_feat: bfloat16 [4096, 256], P('col'), may hold values from -3.5 to 3.5
- source_type: int32 [16384], P('row'), may hold values from 0 to 15
- target_type: int32 [4096], P('col'), may hold values from 0 to 15
- row_weight: float32 [16384], P('row'), may hold values from 0.5 to 10
- col_weight: float32 [4096], P('col'), may hold values from 0.5 to 2
Outputs:
- coupling_next: bfloat16 [16384, 4096], P('row', 'col')
- barycentre: bfloat16 [16384, 256], P(('row', 'col'))
The draws below stay inside these ranges and needn't reach their ends.
Inputs may be any that keep to these rules, and one draw needn't show every extreme that they name: `source_dist`: symmetric.
All inputs are finite; a program needn't handle non-finite values.
Results may differ from the reference program's by a relative error of at most 0.02.
Values may be sent and summed in bfloat16 or wider, within the bound.
A program may use at most 128 MiB of HBM per device.

```python
import math
import jax
import jax.numpy as jnp
from jax import lax

FEAT = 256
TYPES = 16
N_SRC = 16384
N_TGT = 4096


def draw_source_dist(key, part):
    uniform_vals = jax.random.uniform(jax.random.fold_in(key, 21), (N_SRC, N_SRC), jnp.float32, -1.0, 1.0)
    mirrored = jnp.triu(uniform_vals) + jnp.triu(uniform_vals, 1).T
    return (mirrored * (0.99 * (3.0 / N_SRC) ** 0.5)).astype(jnp.bfloat16)


def draw_source_feat(key, part):
    noise = jax.random.normal(jax.random.fold_in(key, 12), (N_SRC, FEAT), jnp.float32)
    values = jnp.clip(noise, -3.5, 3.5)
    return values.astype(jnp.bfloat16)


def draw_target_feat(key, part):
    values = jnp.clip(jax.random.normal(jax.random.fold_in(key, 13), (N_TGT, FEAT), jnp.float32), -3.5, 3.5)
    return values.astype(jnp.bfloat16)


def draw_row_weight(key, part):
    position = jnp.arange(N_SRC, dtype=jnp.float32) / (N_SRC - 1)
    factor = jnp.exp(jax.random.uniform(jax.random.fold_in(key, 31), (N_SRC,), jnp.float32, jnp.log(0.5), jnp.log(2.0)))
    return (1.0 + 2.0 * position) * factor


def plant(drawn, key, smallest, top_value):
    shape = drawn.shape
    place = [jax.random.randint(jax.random.fold_in(key, axis), (), 0, shape[axis]) for axis in range(len(shape))]
    drawn = drawn.at[tuple(place)].set(smallest)
    longest = shape.index(max(shape))
    place[longest] = (place[longest] + 1) % shape[longest]
    return drawn.at[tuple(place)].set(top_value)


def levels(own_key, shape, split, least, largest):
    factor_of = 1.0
    for axis_at, blocks in split:
        draws = jax.random.uniform(jax.random.fold_in(jax.random.fold_in(own_key, 6), axis_at), (blocks,), jnp.float32, least / len(split), largest / len(split))
        factor_of = factor_of * jnp.repeat(jnp.exp(draws), shape[axis_at] // blocks).reshape((-1,) + (1,) * (len(shape) - 1 - axis_at))
    return factor_of


def normal_values(key, dims, spread, bound, split=(), kind=jnp.bfloat16):
    result = spread * jax.random.normal(key, dims, jnp.float32)
    if split:
        result = result * levels(key, dims, split, -0.22, 0.18)
    return jnp.clip(result, -bound, bound).astype(kind)


def setup_inputs(seed: int = 0) -> dict:
    splits = jax.random.split(jax.random.key(seed), 10)
    return {
        "coupling": jnp.clip(jnp.exp(math.log(5.0) - 3.2227897 * jax.random.uniform(splits[0], (N_SRC, N_TGT), jnp.float32) ** levels(splits[0], (N_SRC, N_TGT), ((0, 32), (1, 8)), -0.2, 0.2)), 0.19921875, 5.0).astype(jnp.bfloat16),
        "source_dist": draw_source_dist(jax.random.fold_in(splits[9], 71), 0),
        "target_dist": normal_values(splits[2], (N_TGT, N_TGT), N_TGT ** -0.5, 0.09375, ((0, 32), (1, 8))),
        "source_feat": draw_source_feat(jax.random.fold_in(splits[9], 71), 0),
        "target_feat": draw_target_feat(jax.random.fold_in(splits[9], 71), 0),
        "source_type": plant(jax.random.randint(splits[5], (N_SRC,), 0, TYPES), jax.random.fold_in(splits[5], 1), 0, TYPES - 1).astype(jnp.int32),
        "target_type": plant(jax.random.randint(splits[6], (N_TGT,), 0, TYPES), jax.random.fold_in(splits[6], 1), 0, TYPES - 1).astype(jnp.int32),
        "row_weight": draw_row_weight(jax.random.fold_in(splits[9], 71), 0),
        "col_weight": jnp.clip(jnp.exp(math.log(2.0) - 1.3862944 * jax.random.uniform(splits[8], (N_TGT,), jnp.float32) ** levels(splits[8], (N_TGT,), ((0, 8),), -0.2, 0.2)), 0.5, 2.0),
    }


coupling_weight = 0.5
feature_weight = 2.5
mismatch_cost = 1.0

def log_sum_exp(values, axis):
    highest = lax.optimization_barrier(jnp.max(values, axis=axis, keepdims=True))
    return highest + jnp.log(lax.optimization_barrier(jnp.sum(jnp.exp(values - highest), axis=axis, keepdims=True)))

def exact_dot(left, right):
    return jnp.dot(left.astype(jnp.float32), right.astype(jnp.float32), precision=lax.Precision.HIGHEST, preferred_element_type=jnp.float32)

def reference(coupling, source_dist, target_dist, source_feat, target_feat, source_type, target_type, row_weight, col_weight):
    first = exact_dot(source_dist, coupling).astype(jnp.bfloat16)
    second = exact_dot(first, target_dist)
    affinity = exact_dot(source_feat, target_feat.T)
    mismatch = (source_type[:, None] != target_type[None, :]).astype(jnp.float32)
    score = jnp.log(coupling.astype(jnp.float32)) + coupling_weight * second + feature_weight / math.sqrt(FEAT) * affinity - mismatch_cost * mismatch
    first_log = score - log_sum_exp(score, 1) + jnp.log(row_weight)[:, None] + math.log(N_TGT)
    next_log = first_log - log_sum_exp(first_log, 0) + jnp.log(col_weight)[None, :] + math.log(N_SRC)
    next_float = jnp.exp(next_log)
    coupling_next = next_float.astype(jnp.bfloat16)
    numer = exact_dot(coupling_next, target_feat)
    mass = lax.optimization_barrier(jnp.sum(next_float, axis=1, keepdims=True))
    return (coupling_next, (numer / mass).astype(jnp.bfloat16))
```

```python
import math

import jax
import jax.numpy as jnp
from jax import lax
from jax.experimental import pallas as pl
from jax.experimental.pallas import tpu as pltpu
from jax.sharding import PartitionSpec as P

MESH = pl.DeviceIdType.MESH
F32 = jnp.float32
BF16 = jnp.bfloat16

coupling_weight = 0.5
feature_weight = 2.5
mismatch_cost = 1.0

NZ = 8
NROW = 32
NCOL = 8
B = 512
H = B // 2
TB = 128
SB = B // NCOL
FEAT = 256
RT = 64
DIRS = (1, -1)
GROUPS = [(0, 0)] + [(s, d) for s in (1, 2, 3) for d in DIRS] + [(4, 1)]


def group_id(s, d):
    return GROUPS.index((s, {0: 0, 4: 1}.get(s, d)))


def lanes_to_tile(top, bottom):
    return jnp.concatenate(
        [v[:, k * 128 : (k + 1) * 128] for v in (top, bottom) for k in range(B // 128)], axis=0
    )


def tile_to_lanes(tile):
    return jnp.concatenate([tile[k : k + 1, :] for k in range(B // 128)], axis=1)


def to_sublanes(row):
    return jnp.transpose(jnp.broadcast_to(row, (128, B)))


def kernel(
    coupling,
    source_dist,
    target_dist,
    source_feat,
    target_feat,
    source_type,
    target_type,
    row_weight,
    col_weight,
    next_out,
    bary_out,
    dist,
    cbuf,
    tbuf,
    fbuf,
    acc,
    acc2,
    pre,
    sfeat,
    tfeat,
    stype,
    ttype,
    roww,
    colw,
    stat,
    rstat,
    cstat,
    nxt,
    parts,
    got,
    bary,
    in_sem,
    dist_sem,
    out_sem,
    zs_sem,
    zr_sem,
    ys_sem,
    yr_sem,
    bs_sem,
    br_sem,
    fs_sem,
    fr_sem,
    rs_sem,
    rr_sem,
    cs_sem,
    cr_sem,
    ps_sem,
    pr_sem,
):
    row = lax.axis_index("row")
    col = lax.axis_index("col")
    z = row // 4
    lane = (row // 2) % 2
    core = row % 2
    x = col % 4
    yhi = col // 4

    def row_at(zz, line):
        return zz * 4 + line * 2 + core

    def zpos(s, d):
        return (z + NZ - d * s) % NZ

    z_dev = {d: (((z + NZ + d) % NZ) * 4 + lane * 2 + core, col) for d in DIRS}
    y_dev = (z * 4 + (1 - lane) * 2 + core, col)
    sib_dev = (z * 4 + lane * 2 + 1 - core, col)
    x_dev = {d: (row, yhi * 4 + (x + 4 + d) % 4) for d in DIRS}
    hi_dev = (row, (1 - yhi) * 4 + x)

    own_in = []

    def bring(k, src, dst):
        copy = pltpu.make_async_copy(src, dst, in_sem.at[k])
        copy.start()
        own_in.append(copy)

    mine = pl.ds(pl.multiple_of(row * B, B), B)
    bring(0, coupling.at[:, pl.ds(0, H)], cbuf.at[0, mine])
    bring(1, coupling.at[:, pl.ds(H, H)], cbuf.at[1, mine])
    bring(2, target_dist, tbuf.at[pl.ds(pl.multiple_of(row * TB, TB), TB)])
    bring(3, source_feat, sfeat)
    bring(4, target_feat, tfeat)
    bring(5, source_type, stype)
    bring(6, target_type, ttype)
    bring(7, row_weight, roww)
    bring(8, col_weight, colw)

    def dist_copy(zz):
        span = pl.ds(pl.multiple_of(zz * 4 * B, 4 * B), 4 * B)
        return pltpu.make_async_copy(source_dist.at[:, span], dist.at[:, span], dist_sem.at[zz])

    for g, (s, d) in enumerate(GROUPS):
        dist_copy(zpos(s, d)).start()

    barrier = pltpu.get_barrier_semaphore()
    for j in range(1, NROW):
        pl.semaphore_signal(
            barrier, inc=1, device_id=((row + j) % NROW, col), device_id_type=MESH
        )
    for j in range(1, NCOL):
        pl.semaphore_signal(
            barrier, inc=1, device_id=(row, (col + j) % NCOL), device_id_type=MESH
        )
    pl.semaphore_wait(barrier, NROW - 1 + NCOL - 1)

    started = []

    def remote(src, dst, ssem, rsem, dev):
        return pltpu.make_async_remote_copy(
            src_ref=src,
            dst_ref=dst,
            send_sem=ssem,
            recv_sem=rsem,
            device_id=dev,
            device_id_type=MESH,
        )

    def send(copy):
        copy.start()
        started.append(copy)

    bufs = [cbuf.at[0], cbuf.at[1], tbuf]
    sizes = [B, B, TB]

    def piece(p, origin, part, quarter=None):
        half = sizes[p] // 2
        start = origin * sizes[p] + part * half
        if quarter is None:
            return bufs[p].at[pl.ds(pl.multiple_of(start, half), half)]
        return bufs[p].at[pl.ds(pl.multiple_of(start + quarter * (half // 2), half // 2), half // 2)]

    def whole(p, origin):
        return bufs[p].at[pl.ds(pl.multiple_of(origin * sizes[p], sizes[p]), sizes[p])]

    KIND = [(0, 0), (0, 1), (1, 1)]

    def z_copy(p, kind, s, d, origin_z):
        other, part = KIND[kind]
        line = 1 - lane if other else lane
        quarter = None if s < 4 else (0 if d == 1 else 1)
        ref = piece(p, row_at(origin_z, line), part, quarter)
        n = ((p * 3 + kind) * 2 + (0 if d == 1 else 1)) * 4 + s - 1
        return remote(ref, ref, zs_sem.at[n], zr_sem.at[n], z_dev[d])

    def y_send_copy(p, g, part, incoming):
        s, d = GROUPS[g]
        line = 1 - lane if incoming else lane
        ref = piece(p, row_at(zpos(s, d), line), part)
        n = p * 9 + (8 if part == 1 else g)
        return remote(ref, ref, ys_sem.at[n], yr_sem.at[n], y_dev)

    def sib_copy(p, g, other, incoming):
        s, d = GROUPS[g]
        line = 1 - lane if other else lane
        origin = zpos(s, d) * 4 + line * 2 + (1 - core if incoming else core)
        ref = whole(p, origin)
        n = (p * 8 + g) * 2 + other
        return remote(ref, ref, bs_sem.at[n], br_sem.at[n], sib_dev)

    def z_forward(p, kind, s, d):
        if s < 4:
            send(z_copy(p, kind, s + 1, d, zpos(s, d)))

    def phase_start(p):
        send(y_send_copy(p, 0, 1, False))
        for kind in (1, 0):
            for d in DIRS:
                send(z_copy(p, kind, 1, d, z))
        send(y_send_copy(p, 0, 0, False))
        send(sib_copy(p, 0, 0, False))

    def phase_other(p):
        y_send_copy(p, 0, 1, True).wait_recv()
        for d in DIRS:
            send(z_copy(p, 2, 1, d, z))

    def other_to_sib(p, s):
        for d in DIRS if s in (1, 2, 3) else (0,):
            g = group_id(s, d)
            y_send_copy(p, g, 0, True).wait_recv()
            send(sib_copy(p, g, 1, False))

    def phase_step(p, s):
        for d in DIRS:
            for kind in (1, 0):
                z_copy(p, kind, s, d, zpos(s, d)).wait_recv()
                z_forward(p, kind, s, d)
            if s < 4:
                send(y_send_copy(p, group_id(s, d), 0, False))
                send(sib_copy(p, group_id(s, d), 0, False))
        if s == 4:
            send(y_send_copy(p, group_id(4, 0), 0, False))
            send(sib_copy(p, group_id(4, 0), 0, False))
        for d in DIRS:
            z_copy(p, 2, s, d, zpos(s, d)).wait_recv()
            z_forward(p, 2, s, d)
        other_to_sib(p, s - 1)

    def sib_wait(p, g):
        for other in (0, 1):
            sib_copy(p, g, other, True).wait_recv()

    def groups_at(s):
        return [g for g, (t, _) in enumerate(GROUPS) if t == s]

    def matmul_first(p, s):
        for g in groups_at(s):
            sib_wait(p, g)
            zz = zpos(*GROUPS[g])
            if p == 0:
                dist_copy(zz).wait()

            def body(k, _):
                at = pl.multiple_of(zz * (4 * B) + k * B, B)
                prod = jnp.dot(
                    dist[:, pl.ds(at, B)], cbuf[p, pl.ds(at, B), :], preferred_element_type=F32
                )
                acc[...] += prod
                return 0

            lax.fori_loop(0, 4, body, 0)

    def first_copy(h, at_col, ssem_id, dev, span=None):
        ref = fbuf.at[at_col, h]
        if span is not None:
            ref = ref.at[pl.ds(span * H, H)]
        n = h * 9 + ssem_id
        return remote(ref, ref, fs_sem.at[n], fr_sem.at[n], dev)

    def x_col(y, s, d):
        return y * 4 + (x + 4 - d * s) % 4

    def x_copy(h, other, s, d, origin):
        n = 1 + other * 4 + (s - 1) * 2 + (0 if d == 1 else 1)
        span = None if s == 1 else (0 if d == 1 else 1)
        return first_copy(h, origin, n, x_dev[d], span)

    def gather_first_start(h):
        fbuf[col, h] = acc[...].astype(BF16)
        acc[...] = jnp.zeros_like(acc)
        send(first_copy(h, col, 0, hi_dev))
        for d in DIRS:
            send(x_copy(h, 0, 1, d, col))

    def gather_first_1(h):
        first_copy(h, (1 - yhi) * 4 + x, 0, hi_dev).wait_recv()
        for d in DIRS:
            send(x_copy(h, 1, 1, d, (1 - yhi) * 4 + x))
        for d in DIRS:
            x_copy(h, 0, 1, d, x_col(yhi, 1, d)).wait_recv()
            send(x_copy(h, 0, 2, d, x_col(yhi, 1, d)))

    def gather_first_2(h):
        for d in DIRS:
            x_copy(h, 1, 1, d, x_col(1 - yhi, 1, d)).wait_recv()
            send(x_copy(h, 1, 2, d, x_col(1 - yhi, 1, d)))

    def gather_first_3(h):
        for other in (0, 1):
            for d in DIRS:
                y = 1 - yhi if other else yhi
                x_copy(h, other, 2, d, x_col(y, 2, d)).wait_recv()

    def add_second(zz, h):
        at = pl.multiple_of(zz * B + h * H, H)
        acc2[...] += jnp.dot(fbuf[zz, h], tbuf[pl.ds(at, H), :], preferred_element_type=F32)

    def matmul_second(s):
        for g in groups_at(s):
            sib_wait(2, g)
            add_second(zpos(*GROUPS[g]), 0)

    def row_steps(body):
        lax.fori_loop(0, B // RT, lambda i, _: (body(pl.ds(pl.multiple_of(i * RT, RT), RT)), 0)[1], 0)

    def prepare():
        for copy in own_in[3:]:
            copy.wait()
        acc[...] = jnp.zeros_like(acc)
        acc2[...] = jnp.zeros_like(acc2)
        stat[...] = to_sublanes(stype[...].reshape(1, B).astype(F32))
        kinds = ttype[...].reshape(1, B).astype(F32)

        def body(rows):
            affinity = lax.dot_general(
                sfeat[rows, :], tfeat[...], (((1,), (1,)), ((), ())), preferred_element_type=F32
            )
            for h in range(2):
                base = pl.multiple_of(row * B + rows.start, RT)
                pre[rows, h * H : (h + 1) * H] = jnp.log(
                    cbuf[h, pl.ds(base, RT), :].astype(F32)
                )
            own = stat[rows, :]
            for k in range(B // 128):
                cut = slice(k * 128, (k + 1) * 128)
                mismatch = jnp.where(own != kinds[:, cut], 1.0, 0.0).astype(F32)
                pre[rows, cut] = (
                    pre[rows, cut]
                    + feature_weight / math.sqrt(FEAT) * affinity[:, cut]
                    - mismatch_cost * mismatch
                )

        row_steps(body)

    own_in[0].wait()
    phase_start(0)
    own_in[1].wait()
    own_in[2].wait()
    phase_other(0)
    prepare()
    phase_step(0, 1)
    phase_step(0, 2)
    matmul_first(0, 0)
    phase_step(0, 3)
    phase_start(1)
    matmul_first(0, 1)
    phase_step(0, 4)
    phase_other(1)
    matmul_first(0, 2)
    phase_step(1, 1)
    other_to_sib(0, 4)
    matmul_first(0, 3)
    phase_step(1, 2)
    matmul_first(0, 4)
    gather_first_start(0)
    matmul_first(1, 0)
    phase_step(1, 3)
    phase_start(2)
    gather_first_1(0)
    matmul_first(1, 1)
    phase_step(1, 4)
    phase_other(2)
    gather_first_2(0)
    matmul_first(1, 2)
    other_to_sib(1, 4)
    phase_step(2, 1)
    matmul_first(1, 3)
    matmul_first(1, 4)
    gather_first_start(1)
    phase_step(2, 2)
    gather_first_3(0)
    matmul_second(0)
    phase_step(2, 3)
    gather_first_1(1)
    matmul_second(1)
    phase_step(2, 4)
    gather_first_2(1)
    matmul_second(2)
    other_to_sib(2, 4)
    matmul_second(3)
    matmul_second(4)
    gather_first_3(1)
    lax.fori_loop(0, NCOL, lambda k, _: (add_second(k, 1), 0)[1], 0)

    spot = lax.broadcasted_iota(jnp.int32, (RT, 128), 1)

    def row_stats(rows):
        score = pre[rows, :] + coupling_weight * acc2[rows, :]
        pre[rows, :] = score
        top = jnp.max(score, axis=1, keepdims=True)
        total = jnp.sum(jnp.exp(score - top), axis=1, keepdims=True)
        stat[rows, :] = jnp.where(spot < 64, top, total)

    row_steps(row_stats)
    turned = jnp.transpose(stat[...])
    rstat[col] = lanes_to_tile(turned[0:1, :], turned[64:65, :])
    for j in range(1, NCOL):
        send(
            remote(
                rstat.at[col],
                rstat.at[col],
                rs_sem.at[j],
                rr_sem.at[j],
                (row, (col + j) % NCOL),
            )
        )
    for j in range(1, NCOL):
        came = (col + NCOL - j) % NCOL
        remote(rstat.at[came], rstat.at[came], rs_sem.at[j], rr_sem.at[j], (row, came)).wait_recv()

    def combined(ref):
        tops = ref[:, 0:4, :]
        top = jnp.max(tops, axis=0)
        total = jnp.sum(ref[:, 4:8, :] * jnp.exp(tops - top[None]), axis=0)
        return top + jnp.log(total)

    row_lse = tile_to_lanes(combined(rstat))
    shift = jnp.log(roww[...].reshape(1, B)) + math.log(NCOL * B) - row_lse
    stat[...] = to_sublanes(shift)

    def shifted(rows, best):
        move = stat[rows, :]
        tops = []
        for k in range(B // 128):
            cut = slice(k * 128, (k + 1) * 128)
            value = pre[rows, cut] + move
            pre[rows, cut] = value
            tops.append(jnp.max(value, axis=0, keepdims=True))
        return jnp.maximum(best, jnp.concatenate(tops, axis=1))

    def over_rows(body, start):
        return lax.fori_loop(
            0, B // RT, lambda i, c: body(pl.ds(pl.multiple_of(i * RT, RT), RT), c), start
        )

    col_top = over_rows(shifted, jnp.full((1, B), -jnp.inf, F32))
    col_sum = over_rows(
        lambda rows, c: c + jnp.sum(jnp.exp(pre[rows, :] - col_top), axis=0, keepdims=True),
        jnp.zeros((1, B), F32),
    )
    cstat[row] = lanes_to_tile(col_top, col_sum)
    for j in range(1, NROW):
        send(
            remote(
                cstat.at[row],
                cstat.at[row],
                cs_sem.at[j],
                cr_sem.at[j],
                ((row + j) % NROW, col),
            )
        )
    for j in range(1, NROW):
        came = (row + NROW - j) % NROW
        remote(cstat.at[came], cstat.at[came], cs_sem.at[j], cr_sem.at[j], (came, col)).wait_recv()
    col_shift = (
        jnp.log(colw[...].reshape(1, B)) + math.log(NROW * B) - tile_to_lanes(combined(cstat))
    )

    def finish(rows):
        value = jnp.exp(pre[rows, :] + col_shift)
        rounded = value.astype(BF16)
        nxt[rows, :] = rounded
        parts[rows, 0:FEAT] = jnp.dot(rounded, tfeat[...], preferred_element_type=F32).astype(BF16)
        mass = jnp.sum(value, axis=1, keepdims=True)
        high = mass.astype(BF16).astype(F32)
        parts[rows, FEAT : FEAT + 128] = jnp.where(spot < 64, high, mass - high).astype(BF16)

    row_steps(finish)
    out_copy = pltpu.make_async_copy(nxt, next_out, out_sem.at[0])
    out_copy.start()

    def part_of(c):
        return parts.at[pl.ds(pl.multiple_of(c * SB, SB), SB)]

    for j in range(1, NCOL):
        goes = (col + j) % NCOL
        send(remote(part_of(goes), got.at[col], ps_sem.at[j], pr_sem.at[j], (row, goes)))
    total = parts[pl.ds(pl.multiple_of(col * SB, SB), SB), :].astype(F32)
    for j in range(1, NCOL):
        came = (col + NCOL - j) % NCOL
        remote(part_of(came), got.at[came], ps_sem.at[j], pr_sem.at[j], (row, came)).wait_recv()
        total = total + got[came].astype(F32)
    mass = total[:, FEAT : FEAT + 1] + total[:, FEAT + 64 : FEAT + 65]
    bary[...] = (total[:, 0:FEAT] / mass).astype(BF16)
    bary_copy = pltpu.make_async_copy(bary, bary_out, out_sem.at[1])
    bary_copy.start()

    for copy in started:
        copy.wait_send()
    out_copy.wait()
    bary_copy.wait()


def shards(*args):
    anywhere = pl.BlockSpec(memory_space=pl.ANY)
    dma = pltpu.SemaphoreType.DMA
    return tuple(
        pl.pallas_call(
            kernel,
            out_shape=(
                jax.ShapeDtypeStruct((B, B), BF16),
                jax.ShapeDtypeStruct((SB, FEAT), BF16),
            ),
            in_specs=[anywhere] * 9,
            out_specs=(anywhere, anywhere),
            scratch_shapes=[
                pltpu.VMEM((B, NROW * B), BF16),
                pltpu.VMEM((2, NROW * B, H), BF16),
                pltpu.VMEM((NROW * TB, B), BF16),
                pltpu.VMEM((NCOL, 2, B, H), BF16),
                pltpu.VMEM((B, H), F32),
                pltpu.VMEM((B, B), F32),
                pltpu.VMEM((B, B), F32),
                pltpu.VMEM((B, FEAT), BF16),
                pltpu.VMEM((B, FEAT), BF16),
                pltpu.VMEM((B,), jnp.int32),
                pltpu.VMEM((B,), jnp.int32),
                pltpu.VMEM((B,), F32),
                pltpu.VMEM((B,), F32),
                pltpu.VMEM((B, 128), F32),
                pltpu.VMEM((NCOL, 8, 128), F32),
                pltpu.VMEM((NROW, 8, 128), F32),
                pltpu.VMEM((B, B), BF16),
                pltpu.VMEM((B, FEAT + 128), BF16),
                pltpu.VMEM((NCOL, SB, FEAT + 128), BF16),
                pltpu.VMEM((SB, FEAT), BF16),
                dma((9,)),
                dma((NZ,)),
                dma((2,)),
                dma((72,)),
                dma((72,)),
                dma((27,)),
                dma((27,)),
                dma((48,)),
                dma((48,)),
                dma((18,)),
                dma((18,)),
                dma((NCOL,)),
                dma((NCOL,)),
                dma((NROW,)),
                dma((NROW,)),
                dma((NCOL,)),
                dma((NCOL,)),
            ],
            compiler_params=pltpu.CompilerParams(
                collective_id=0, has_side_effects=True, vmem_limit_bytes=60 * 2**20
            ),
            name="mirror_step",
        )(*args)
    )


def solution(mesh):
    in_specs = (
        P("row", "col"),
        P("row", None),
        P("row", "col"),
        P("row", None),
        P("col", None),
        P("row"),
        P("col"),
        P("row"),
        P("col"),
    )
    out_specs = (P("row", "col"), P(("row", "col"), None))
    return jax.shard_map(shards, mesh=mesh, in_specs=in_specs, out_specs=out_specs, check_vma=False)
```

```python
import functools
import math

import jax
import jax.numpy as jnp
from jax import lax
from jax.experimental import pallas as pl
from jax.experimental.pallas import tpu as pltpu
from jax.sharding import PartitionSpec as P

MESH = pl.DeviceIdType.MESH
F32 = jnp.float32
BF16 = jnp.bfloat16

coupling_weight = 0.5
feature_weight = 2.5
mismatch_cost = 1.0

NZ = 8
NROW = 32
NCOL = 8
B = 512
NP = 2
R = B // NP
Q = R // 4
TB = 128
SB = B // NCOL
FEAT = 256
RT = 64
DIRS = (1, -1)
GROUPS = [(0, 0)] + [(s, d) for s in (1, 2, 3) for d in DIRS] + [(4, 1)]


def group_id(s, d):
    return GROUPS.index((s, {0: 0, 4: 1}.get(s, d)))


def lanes_to_tile(top, bottom):
    return jnp.concatenate(
        [v[:, k * 128 : (k + 1) * 128] for v in (top, bottom) for k in range(B // 128)], axis=0
    )


def tile_to_lanes(tile):
    return jnp.concatenate([tile[k : k + 1, :] for k in range(B // 128)], axis=1)


def to_sublanes(row):
    return jnp.transpose(jnp.broadcast_to(row, (128, B)))


def kernel(
    coupling,
    source_dist,
    target_dist,
    source_feat,
    target_feat,
    source_type,
    target_type,
    row_weight,
    col_weight,
    next_hbm,
    bary_hbm,
    dist,
    tbuf,
    gbuf,
    fbuf,
    acc,
    second,
    pre,
    sfeat,
    tfeat,
    stype,
    ttype,
    roww,
    colw,
    stat,
    rstat,
    cstat,
    next_out,
    bary_out,
    parts,
    got,
    in_sem,
    dist_sem,
    out_sem,
    zs_sem,
    zr_sem,
    ys_sem,
    yr_sem,
    bs_sem,
    br_sem,
    fs_sem,
    fr_sem,
    rs_sem,
    rr_sem,
    cs_sem,
    cr_sem,
    ps_sem,
    pr_sem,
):
    row = lax.axis_index("row")
    col = lax.axis_index("col")
    z = row // 4
    lane = (row // 2) % 2
    core = row % 2
    x = col % 4
    yhi = col // 4

    def row_at(zz, line):
        return zz * 4 + line * 2 + core

    def zpos(s, d):
        return (z + NZ - d * s) % NZ

    z_dev = {d: (((z + NZ + d) % NZ) * 4 + lane * 2 + core, col) for d in DIRS}
    y_dev = (z * 4 + (1 - lane) * 2 + core, col)
    sib_dev = (z * 4 + lane * 2 + 1 - core, col)
    x_dev = {d: (row, yhi * 4 + (x + 4 + d) % 4) for d in DIRS}
    hi_dev = (row, (1 - yhi) * 4 + x)

    barrier = pltpu.get_barrier_semaphore()
    near = (*z_dev.values(), y_dev, sib_dev, *x_dev.values(), hi_dev)
    for dev in near:
        pl.semaphore_signal(barrier, inc=1, device_id=dev, device_id_type=MESH)
    own_in = []

    def bring(k, src, dst):
        copy = pltpu.make_async_copy(src, dst, in_sem.at[k])
        copy.start()
        own_in.append(copy)

    for m in range(NP):
        bring(m, coupling.at[pl.ds(m * R, R)], fbuf.at[m, col])
    own_rows = pl.ds(pl.multiple_of(row * TB, TB), TB)
    bring(NP, target_dist, tbuf.at[own_rows])
    bring(3, source_feat, sfeat)
    bring(4, target_feat, tfeat)
    bring(5, source_type, stype)
    bring(6, target_type, ttype)
    bring(7, row_weight, roww)
    bring(8, col_weight, colw)

    def dist_copy(m, zz, k):
        origin = zz * 4 + k
        src = pl.ds(pl.multiple_of(origin * B + m * R, R), R)
        dst = pl.ds(pl.multiple_of(origin * R, R), R)
        return pltpu.make_async_copy(
            source_dist.at[:, src], dist.at[m, :, dst], dist_sem.at[m * NROW + origin]
        )

    pl.semaphore_wait(barrier, len(near))

    started = []

    def remote(src, dst, ssem, rsem, dev):
        return pltpu.make_async_remote_copy(
            src_ref=src,
            dst_ref=dst,
            send_sem=ssem,
            recv_sem=rsem,
            device_id=dev,
            device_id_type=MESH,
        )

    def send(copy):
        copy.start()
        started.append(copy)

    bufs = [tbuf] + [gbuf.at[m] for m in range(NP)]
    sizes = [TB] + [R] * NP

    def piece(p, origin, part, quarter=None):
        half = sizes[p] // 2
        start = origin * sizes[p] + part * half
        if quarter is None:
            return bufs[p].at[pl.ds(pl.multiple_of(start, half), half)]
        return bufs[p].at[pl.ds(pl.multiple_of(start + quarter * (half // 2), half // 2), half // 2)]

    def whole(p, origin):
        return bufs[p].at[pl.ds(pl.multiple_of(origin * sizes[p], sizes[p]), sizes[p])]

    KIND = [(0, 0), (0, 1), (1, 1)]

    def z_copy(p, kind, s, d, origin_z):
        other, part = KIND[kind]
        line = 1 - lane if other else lane
        quarter = None if s < 4 else (0 if d == 1 else 1)
        ref = piece(p, row_at(origin_z, line), part, quarter)
        n = ((p * 3 + kind) * 2 + (0 if d == 1 else 1)) * 4 + s - 1
        return remote(ref, ref, zs_sem.at[n], zr_sem.at[n], z_dev[d])

    def y_send_copy(p, g, part, incoming):
        s, d = GROUPS[g]
        line = 1 - lane if incoming else lane
        ref = piece(p, row_at(zpos(s, d), line), part)
        n = p * 9 + (8 if part == 1 else g)
        return remote(ref, ref, ys_sem.at[n], yr_sem.at[n], y_dev)

    def sib_copy(p, g, other, incoming):
        s, d = GROUPS[g]
        line = 1 - lane if other else lane
        origin = zpos(s, d) * 4 + line * 2 + (1 - core if incoming else core)
        ref = whole(p, origin)
        n = (p * 8 + g) * 2 + other
        return remote(ref, ref, bs_sem.at[n], br_sem.at[n], sib_dev)

    def z_forward(p, kind, s, d):
        if s < 4:
            send(z_copy(p, kind, s + 1, d, zpos(s, d)))

    def phase_start(ps, then=lambda: None):
        for p in ps:
            send(y_send_copy(p, 0, 1, False))
        then()
        for kind in (0, 1):
            for p in ps:
                for d in DIRS:
                    send(z_copy(p, kind, 1, d, z))
        for p in ps:
            send(y_send_copy(p, 0, 0, False))
            send(sib_copy(p, 0, 0, False))

    def phase_other(ps):
        for p in ps:
            y_send_copy(p, 0, 1, True).wait_recv()
            for d in DIRS:
                send(z_copy(p, 2, 1, d, z))

    def other_to_sib(ps, s):
        for p in ps:
            for d in DIRS if s in (1, 2, 3) else (0,):
                g = group_id(s, d)
                y_send_copy(p, g, 0, True).wait_recv()
                send(sib_copy(p, g, 1, False))

    work = []

    def do_some(count=1):
        for _ in range(min(count, len(work))):
            work.pop(0)()

    def do_all():
        do_some(len(work))

    def phase_step(ps, s, count=1):
        for kind in (0, 1, 2):
            for p in ps:
                for d in DIRS:
                    z_copy(p, kind, s, d, zpos(s, d)).wait_recv()
                    z_forward(p, kind, s, d)
                    if kind == 0 and s < 4:
                        send(y_send_copy(p, group_id(s, d), 0, False))
                    if kind == 1 and s < 4:
                        send(sib_copy(p, group_id(s, d), 0, False))
                    do_some(count)
                if kind == 0 and s == 4:
                    send(y_send_copy(p, group_id(4, 0), 0, False))
                if kind == 1 and s == 4:
                    send(sib_copy(p, group_id(4, 0), 0, False))
        other_to_sib(ps, s - 1)

    def sib_wait(p, g):
        for other in (0, 1):
            sib_copy(p, g, other, True).wait_recv()

    def groups_at(s):
        return [g for g, (t, _) in enumerate(GROUPS) if t == s]

    def matmul_piece(p, g, at):
        m = p - 1
        zz = zpos(*GROUPS[g])
        if at == 0:
            sib_wait(p, g)
            for k in range(4):
                dist_copy(m, zz, k).wait()
        rows = pl.ds(pl.multiple_of(zz * (4 * R) + at * B, B), B)
        second[...] += jnp.dot(dist[m, :, rows], gbuf[m, rows, :], preferred_element_type=F32)

    def matmul(p, s):
        for g in groups_at(s):
            for at in range(4 * R // B):
                work.append(functools.partial(matmul_piece, p, g, at))

    def first_copy(m, n, at_col, dev, start, size):
        ref = fbuf.at[m, at_col, pl.ds(start, size)]
        n = m * 22 + n
        return remote(ref, ref, fs_sem.at[n], fr_sem.at[n], dev)

    def x_col(other, s, d):
        y = 1 - yhi if other else yhi
        return y * 4 + (x + 4 - d * s) % 4

    def way(d):
        return 0 if d == 1 else 1

    hi_col = (1 - yhi) * 4 + x

    def hi_copy(m, q, at_col):
        return first_copy(m, q, at_col, hi_dev, q * Q, Q)

    def own_copy(m, s, d, at_col):
        n = 4 + (s - 1) * 2 + way(d)
        if s == 1:
            return first_copy(m, n, at_col, x_dev[d], 0, R)
        return first_copy(m, n, at_col, x_dev[d], way(d) * 2 * Q, 2 * Q)

    def other_copy(m, q, s, d, at_col):
        n = 8 + q * 2 + way(d) if s == 1 else 16 + q
        return first_copy(m, n, at_col, x_dev[d], q * Q, Q)

    def hi_send(m, q):
        send(hi_copy(m, q, col))

    def own_send(m):
        for d in DIRS:
            send(own_copy(m, 1, d, col))

    def own_pass(m):
        for d in DIRS:
            own_copy(m, 1, d, x_col(0, 1, d)).wait_recv()
            send(own_copy(m, 2, d, x_col(0, 1, d)))

    def own_end(m):
        for d in DIRS:
            own_copy(m, 2, d, x_col(0, 2, d)).wait_recv()

    def hi_pass(m, q):
        hi_copy(m, q, hi_col).wait_recv()
        for d in DIRS:
            send(other_copy(m, q, 1, d, hi_col))

    def other_pass(m, q):
        for d in DIRS:
            other_copy(m, q, 1, d, x_col(1, 1, d)).wait_recv()
        d = 1 if q < 2 else -1
        send(other_copy(m, q, 2, d, x_col(1, 1, d)))

    def other_end(m):
        for q in range(4):
            d = 1 if q < 2 else -1
            other_copy(m, q, 2, d, x_col(1, 2, d)).wait_recv()

    def multiply(m, c):
        rows = pl.ds(pl.multiple_of(c * B, B), B)
        acc[m] += jnp.dot(fbuf[m, c], tbuf[rows, :], preferred_element_type=F32)

    def multiply_group(m, g):
        sib_wait(0, g)
        multiply(m, zpos(*GROUPS[g]))

    def keep(m):
        piece_rows = pl.ds(pl.multiple_of(row * R, R), R)
        gbuf[m, piece_rows, :] = acc[m].astype(BF16)

    def build_line(m, other, steps):
        base = (1 - yhi if other else yhi) * 4
        for k in steps:
            work.append(functools.partial(multiply, m, base + (x + k) % 4))

    def build_groups(m, s):
        for g in groups_at(s):
            work.append(functools.partial(multiply_group, m, g))

    def prepare_start():
        for copy in own_in[NP + 1 :]:
            copy.wait()
        stat[...] = to_sublanes(stype[...].reshape(1, B).astype(F32))

    def prepare(m, at):
        kinds = ttype[...].reshape(1, B).astype(F32)
        rows = pl.ds(m * R + at, RT)
        affinity = lax.dot_general(
            sfeat[rows, :], tfeat[...], (((1,), (1,)), ((), ())), preferred_element_type=F32
        )
        base = jnp.log(fbuf[m, col, pl.ds(at, RT), :].astype(F32))
        own = stat[rows, :]
        for k in range(B // 128):
            cut = slice(k * 128, (k + 1) * 128)
            mismatch = jnp.where(own != kinds[:, cut], 1.0, 0.0).astype(F32)
            pre[rows, cut] = (
                base[:, cut]
                + feature_weight / math.sqrt(FEAT) * affinity[:, cut]
                - mismatch_cost * mismatch
            )

    later = functools.partial
    td, g0, g1 = ((p,) for p in range(3))
    own_in[0].wait()
    own_in[NP].wait()
    phase_start(td, later(hi_send, 0, 0))
    own_send(0)
    for m in range(NP):
        for s, d in GROUPS:
            for k in range(4):
                dist_copy(m, zpos(s, d), k).start()
    for ref in (acc, second):
        ref[...] = jnp.zeros_like(ref)
    phase_other(td)
    hi_send(0, 1)
    work.append(later(own_pass, 0))
    work.append(later(hi_pass, 0, 0))
    phase_step(td, 1)
    hi_send(0, 2)
    work.append(later(hi_pass, 0, 1))
    work.append(later(other_pass, 0, 0))
    phase_step(td, 2)
    hi_send(0, 3)
    work.append(later(hi_pass, 0, 2))
    work.append(later(other_pass, 0, 1))
    work.append(later(own_end, 0))
    phase_step(td, 3)
    work.append(later(hi_pass, 0, 3))
    work.append(later(other_pass, 0, 2))
    phase_step(td, 4)
    do_all()
    other_to_sib(td, 4)
    own_in[1].wait()
    other_pass(0, 3)
    hi_send(1, 0)
    own_send(1)
    other_end(0)
    for s in range(5):
        build_groups(0, s)
    work.append(later(keep, 0))
    do_all()
    phase_start(g0)
    hi_send(1, 1)
    prepare_start()
    for at in range(0, R, RT):
        work.append(later(prepare, 0, at))
    phase_other(g0)
    hi_send(1, 2)
    own_pass(1)
    hi_pass(1, 0)
    work.append(later(hi_pass, 1, 1))
    for at in range(0, R, RT):
        work.append(later(prepare, 1, at))
    phase_step(g0, 1)
    hi_send(1, 3)
    work.append(later(other_pass, 1, 0))
    work.append(later(hi_pass, 1, 2))
    work.append(later(own_end, 1))
    build_line(1, 0, range(4))
    phase_step(g0, 2, 2)
    work.append(later(other_pass, 1, 1))
    work.append(later(hi_pass, 1, 3))
    work.append(later(other_pass, 1, 2))
    build_line(1, 1, (0,))
    work.append(later(other_pass, 1, 3))
    build_line(1, 1, (1, 3))
    phase_step(g0, 3, 2)
    do_all()
    other_end(1)
    build_line(1, 1, (2,))
    work.append(later(keep, 1))
    do_all()
    phase_start(g1)
    matmul(1, 0)
    matmul(1, 1)
    phase_step(g0, 4)
    do_all()
    phase_other(g1)
    matmul(1, 2)
    work.insert(2, later(other_to_sib, g0, 4))
    phase_step(g1, 1)
    matmul(1, 3)
    matmul(1, 4)
    phase_step(g1, 2, 2)
    matmul(2, 0)
    phase_step(g1, 3, 2)
    matmul(2, 1)
    phase_step(g1, 4)
    do_some(2)
    other_to_sib(g1, 4)
    matmul(2, 2)
    matmul(2, 3)
    matmul(2, 4)
    do_all()

    def row_steps(body):
        lax.fori_loop(0, B // RT, lambda i, _: (body(pl.ds(pl.multiple_of(i * RT, RT), RT)), 0)[1], 0)

    spot = lax.broadcasted_iota(jnp.int32, (RT, 128), 1)

    def row_stats(rows):
        score = pre[rows, :] + coupling_weight * second[rows, :]
        pre[rows, :] = score
        top = jnp.max(score, axis=1, keepdims=True)
        total = jnp.sum(jnp.exp(score - top), axis=1, keepdims=True)
        stat[rows, :] = jnp.where(spot < 64, top, total)

    row_steps(row_stats)
    turned = jnp.transpose(stat[...])
    rstat[col] = lanes_to_tile(turned[0:1, :], turned[64:65, :])
    for j in range(1, NCOL):
        send(
            remote(
                rstat.at[col],
                rstat.at[col],
                rs_sem.at[j],
                rr_sem.at[j],
                (row, (col + j) % NCOL),
            )
        )
    for j in range(1, NCOL):
        came = (col + NCOL - j) % NCOL
        remote(rstat.at[came], rstat.at[came], rs_sem.at[j], rr_sem.at[j], (row, came)).wait_recv()

    def combined(ref):
        tops = ref[:, 0:4, :]
        top = jnp.max(tops, axis=0)
        total = jnp.sum(ref[:, 4:8, :] * jnp.exp(tops - top[None]), axis=0)
        return top + jnp.log(total)

    row_lse = tile_to_lanes(combined(rstat))
    shift = jnp.log(roww[...].reshape(1, B)) + math.log(NCOL * B) - row_lse
    stat[...] = to_sublanes(shift)

    def shifted(rows, best):
        move = stat[rows, :]
        tops = []
        for k in range(B // 128):
            cut = slice(k * 128, (k + 1) * 128)
            value = pre[rows, cut] + move
            pre[rows, cut] = value
            tops.append(jnp.max(value, axis=0, keepdims=True))
        return jnp.maximum(best, jnp.concatenate(tops, axis=1))

    def over_rows(body, start):
        return lax.fori_loop(
            0, B // RT, lambda i, c: body(pl.ds(pl.multiple_of(i * RT, RT), RT), c), start
        )

    col_top = over_rows(shifted, jnp.full((1, B), -jnp.inf, F32))
    col_sum = over_rows(
        lambda rows, c: c + jnp.sum(jnp.exp(pre[rows, :] - col_top), axis=0, keepdims=True),
        jnp.zeros((1, B), F32),
    )
    cstat[row] = lanes_to_tile(col_top, col_sum)
    for j in range(1, NROW):
        send(
            remote(
                cstat.at[row],
                cstat.at[row],
                cs_sem.at[j],
                cr_sem.at[j],
                ((row + j) % NROW, col),
            )
        )
    for j in range(1, NROW):
        came = (row + NROW - j) % NROW
        remote(cstat.at[came], cstat.at[came], cs_sem.at[j], cr_sem.at[j], (came, col)).wait_recv()
    col_shift = (
        jnp.log(colw[...].reshape(1, B)) + math.log(NROW * B) - tile_to_lanes(combined(cstat))
    )

    def part_of(c):
        return parts.at[pl.ds(pl.multiple_of(c * SB, SB), SB)]

    for j in (6, 2, 5, 7, 4, 3, 1, 0):
        goes = (col + j) % NCOL
        rows = pl.ds(pl.multiple_of(goes * SB, SB), SB)
        value = jnp.exp(pre[rows, :] + col_shift)
        rounded = value.astype(BF16)
        next_out[rows, :] = rounded
        parts[rows, 0:FEAT] = jnp.dot(rounded, tfeat[...], preferred_element_type=F32).astype(BF16)
        mass = jnp.sum(value, axis=1, keepdims=True)
        high = mass.astype(BF16).astype(F32)
        parts[rows, FEAT : FEAT + 128] = jnp.where(spot < 64, high, mass - high).astype(BF16)
        if j:
            send(remote(part_of(goes), got.at[col], ps_sem.at[j], pr_sem.at[j], (row, goes)))
    out_copy = pltpu.make_async_copy(next_out, next_hbm, out_sem.at[0])
    out_copy.start()

    total = parts[pl.ds(pl.multiple_of(col * SB, SB), SB), :].astype(F32)
    for j in range(1, NCOL):
        came = (col + NCOL - j) % NCOL
        remote(part_of(came), got.at[came], ps_sem.at[j], pr_sem.at[j], (row, came)).wait_recv()
        total = total + got[came].astype(F32)
    mass = total[:, FEAT : FEAT + 1] + total[:, FEAT + 64 : FEAT + 65]
    bary_out[...] = (total[:, 0:FEAT] / mass).astype(BF16)
    bary_copy = pltpu.make_async_copy(bary_out, bary_hbm, out_sem.at[1])
    bary_copy.start()

    for copy in started:
        copy.wait_send()
    out_copy.wait()
    bary_copy.wait()


def hand_over(next_in, bary_in, next_out, bary_out, sem):
    copies = (
        pltpu.make_async_copy(next_in, next_out, sem.at[0]),
        pltpu.make_async_copy(bary_in, bary_out, sem.at[1]),
    )
    for copy in copies:
        copy.start()
    for copy in copies:
        copy.wait()


def shards(*args):
    anywhere = pl.BlockSpec(memory_space=pl.ANY)
    dma = pltpu.SemaphoreType.DMA
    results = (
        pl.pallas_call(
            kernel,
            out_shape=(
                jax.ShapeDtypeStruct((B, B), BF16),
                jax.ShapeDtypeStruct((SB, FEAT), BF16),
            ),
            in_specs=[anywhere] * 9,
            out_specs=(anywhere, anywhere),
            scratch_shapes=[
                pltpu.VMEM((NP, B, NROW * R), BF16),
                pltpu.VMEM((NROW * TB, B), BF16),
                pltpu.VMEM((NP, NROW * R, B), BF16),
                pltpu.VMEM((NP, NCOL, R, B), BF16),
                pltpu.VMEM((NP, R, B), F32),
                pltpu.VMEM((B, B), F32),
                pltpu.VMEM((B, B), F32),
                pltpu.VMEM((B, FEAT), BF16),
                pltpu.VMEM((B, FEAT), BF16),
                pltpu.VMEM((B,), jnp.int32),
                pltpu.VMEM((B,), jnp.int32),
                pltpu.VMEM((B,), F32),
                pltpu.VMEM((B,), F32),
                pltpu.VMEM((B, 128), F32),
                pltpu.VMEM((NCOL, 8, 128), F32),
                pltpu.VMEM((NROW, 8, 128), F32),
                pltpu.VMEM((B, B), BF16),
                pltpu.VMEM((SB, FEAT), BF16),
                pltpu.VMEM((B, FEAT + 128), BF16),
                pltpu.VMEM((NCOL, SB, FEAT + 128), BF16),
                dma((NP + 7,)),
                dma((NP * NROW,)),
                dma((2,)),
                dma((72,)),
                dma((72,)),
                dma((27,)),
                dma((27,)),
                dma((48,)),
                dma((48,)),
                dma((44,)),
                dma((44,)),
                dma((NCOL,)),
                dma((NCOL,)),
                dma((NROW,)),
                dma((NROW,)),
                dma((NCOL,)),
                dma((NCOL,)),
            ],
            compiler_params=pltpu.CompilerParams(
                collective_id=0, has_side_effects=True, vmem_limit_bytes=60 * 2**20
            ),
            name="mirror_step",
        )(*args)
    )
    return tuple(
        pl.pallas_call(
            hand_over,
            out_shape=tuple(jax.ShapeDtypeStruct(r.shape, r.dtype) for r in results),
            in_specs=[pl.BlockSpec(memory_space=pltpu.VMEM)] * 2,
            out_specs=(anywhere, anywhere),
            scratch_shapes=[dma((2,))],
            name="hand_over",
        )(*results)
    )


def solution(mesh):
    in_specs = (
        P("row", "col"),
        P("row", None),
        P("row", "col"),
        P("row", None),
        P("col", None),
        P("row"),
        P("col"),
        P("row"),
        P("col"),
    )
    out_specs = (P("row", "col"), P(("row", "col"), None))
    return jax.shard_map(shards, mesh=mesh, in_specs=in_specs, out_specs=out_specs, check_vma=False)
```

```python
import functools
import math

import jax
import jax.numpy as jnp
from jax import lax
from jax.experimental import pallas as pl
from jax.experimental.pallas import tpu as pltpu
from jax.sharding import PartitionSpec as P

MESH = pl.DeviceIdType.MESH
F32 = jnp.float32
BF16 = jnp.bfloat16

coupling_weight = 0.5
feature_weight = 2.5
mismatch_cost = 1.0

NZ = 8
NROW = 32
NCOL = 8
B = 512
NP = 2
R = B // NP
Q = R // 4
TB = 128
SB = B // NCOL
FEAT = 256
RT = 64
RS = 128
DIRS = (1, -1)
GROUPS = [(0, 0)] + [(s, d) for s in (1, 2, 3) for d in DIRS] + [(4, 1)]


def group_id(s, d):
    return GROUPS.index((s, {0: 0, 4: 1}.get(s, d)))


def lanes_to_tile(top, bottom):
    return jnp.concatenate(
        [v[:, k * 128 : (k + 1) * 128] for v in (top, bottom) for k in range(B // 128)], axis=0
    )


def tile_to_lanes(tile):
    return jnp.concatenate([tile[k : k + 1, :] for k in range(B // 128)], axis=1)


def to_sublanes(row):
    return jnp.transpose(jnp.broadcast_to(row, (128, B)))


def kernel(
    coupling,
    source_dist,
    target_dist,
    source_feat,
    target_feat,
    source_type,
    target_type,
    row_weight,
    col_weight,
    next_hbm,
    bary_hbm,
    dist,
    tbuf,
    gbuf,
    fbuf,
    acc,
    second,
    pre,
    sfeat,
    tfeat,
    stype,
    ttype,
    roww,
    colw,
    stat,
    rstat,
    cstat,
    next_out,
    bary_out,
    parts,
    got,
    in_sem,
    dist_sem,
    out_sem,
    zs_sem,
    zr_sem,
    ys_sem,
    yr_sem,
    bs_sem,
    br_sem,
    fs_sem,
    fr_sem,
    rs_sem,
    rr_sem,
    cs_sem,
    cr_sem,
    ps_sem,
    pr_sem,
):
    row = lax.axis_index("row")
    col = lax.axis_index("col")
    z = row // 4
    lane = (row // 2) % 2
    core = row % 2
    x = col % 4
    yhi = col // 4

    def row_at(zz, line):
        return zz * 4 + line * 2 + core

    def zpos(s, d):
        return (z + NZ - d * s) % NZ

    z_dev = {d: (((z + NZ + d) % NZ) * 4 + lane * 2 + core, col) for d in DIRS}
    y_dev = (z * 4 + (1 - lane) * 2 + core, col)
    sib_dev = (z * 4 + lane * 2 + 1 - core, col)
    x_dev = {d: (row, yhi * 4 + (x + 4 + d) % 4) for d in DIRS}
    hi_dev = (row, (1 - yhi) * 4 + x)

    barrier = pltpu.get_barrier_semaphore()
    near = (*z_dev.values(), y_dev, sib_dev, *x_dev.values(), hi_dev)
    for dev in near:
        pl.semaphore_signal(barrier, inc=1, device_id=dev, device_id_type=MESH)
    own_in = []

    def bring(k, src, dst):
        copy = pltpu.make_async_copy(src, dst, in_sem.at[k])
        copy.start()
        own_in.append(copy)

    for m in range(NP):
        bring(m, coupling.at[pl.ds(m * R, R)], fbuf.at[m, col])
    own_rows = pl.ds(pl.multiple_of(row * TB, TB), TB)
    bring(NP, target_dist, tbuf.at[own_rows])
    bring(3, source_feat, sfeat)
    bring(4, target_feat, tfeat)
    bring(5, source_type, stype)
    bring(6, target_type, ttype)
    bring(7, row_weight, roww)
    bring(8, col_weight, colw)

    def dist_copy(m, zz, k):
        origin = zz * 4 + k
        src = pl.ds(pl.multiple_of(origin * B + m * R, R), R)
        dst = pl.ds(pl.multiple_of(origin * R, R), R)
        return pltpu.make_async_copy(
            source_dist.at[:, src], dist.at[m, :, dst], dist_sem.at[m * NROW + origin]
        )

    pl.semaphore_wait(barrier, len(near))

    started = []

    def remote(src, dst, ssem, rsem, dev):
        return pltpu.make_async_remote_copy(
            src_ref=src,
            dst_ref=dst,
            send_sem=ssem,
            recv_sem=rsem,
            device_id=dev,
            device_id_type=MESH,
        )

    def send(copy):
        copy.start()
        started.append(copy)

    bufs = [tbuf] + [gbuf.at[m] for m in range(NP)]
    sizes = [TB] + [R] * NP
    fronts = [TB // 4] + [R // 2] * NP

    def piece(p, origin, part, quarter=None):
        size = sizes[p] - fronts[p] if part else fronts[p]
        start = origin * sizes[p] + part * fronts[p]
        if quarter is not None:
            size //= 2
            start = start + quarter * size
        return bufs[p].at[pl.ds(pl.multiple_of(start, 16), size)]

    def whole(p, origin):
        return bufs[p].at[pl.ds(pl.multiple_of(origin * sizes[p], sizes[p]), sizes[p])]

    KIND = [(0, 0), (0, 1), (1, 1)]

    def z_copy(p, kind, s, d, origin_z):
        other, part = KIND[kind]
        line = 1 - lane if other else lane
        quarter = None if s < 4 else (0 if d == 1 else 1)
        ref = piece(p, row_at(origin_z, line), part, quarter)
        n = ((p * 3 + kind) * 2 + (0 if d == 1 else 1)) * 4 + s - 1
        return remote(ref, ref, zs_sem.at[n], zr_sem.at[n], z_dev[d])

    def y_send_copy(p, g, part, incoming):
        s, d = GROUPS[g]
        line = 1 - lane if incoming else lane
        ref = piece(p, row_at(zpos(s, d), line), part)
        n = p * 9 + (8 if part == 1 else g)
        return remote(ref, ref, ys_sem.at[n], yr_sem.at[n], y_dev)

    def sib_copy(p, g, other, incoming):
        s, d = GROUPS[g]
        line = 1 - lane if other else lane
        origin = zpos(s, d) * 4 + line * 2 + (1 - core if incoming else core)
        ref = whole(p, origin)
        n = (p * 8 + g) * 2 + other
        return remote(ref, ref, bs_sem.at[n], br_sem.at[n], sib_dev)

    def z_forward(p, kind, s, d):
        if s < 4:
            send(z_copy(p, kind, s + 1, d, zpos(s, d)))

    def phase_start(ps, then=lambda: None):
        for p in ps:
            send(y_send_copy(p, 0, 1, False))
        then()
        for kind in (0, 1):
            for p in ps:
                for d in DIRS:
                    send(z_copy(p, kind, 1, d, z))
        for p in ps:
            send(y_send_copy(p, 0, 0, False))
            send(sib_copy(p, 0, 0, False))

    def phase_other(ps):
        for p in ps:
            y_send_copy(p, 0, 1, True).wait_recv()
            for d in DIRS:
                send(z_copy(p, 2, 1, d, z))

    def other_to_sib(ps, s):
        for p in ps:
            for d in DIRS if s in (1, 2, 3) else (0,):
                g = group_id(s, d)
                y_send_copy(p, g, 0, True).wait_recv()
                send(sib_copy(p, g, 1, False))

    work = []

    def do_some(count=1):
        for _ in range(min(count, len(work))):
            work.pop(0)()

    def do_all():
        do_some(len(work))

    def phase_step(ps, s, count=1):
        for kind in (0, 1, 2):
            for p in ps:
                for d in DIRS:
                    z_copy(p, kind, s, d, zpos(s, d)).wait_recv()
                    z_forward(p, kind, s, d)
                    if kind == 0 and s < 4:
                        send(y_send_copy(p, group_id(s, d), 0, False))
                    if kind == 1 and s < 4:
                        send(sib_copy(p, group_id(s, d), 0, False))
                    do_some(count)
                if kind == 0 and s == 4:
                    send(y_send_copy(p, group_id(4, 0), 0, False))
                if kind == 1 and s == 4:
                    send(sib_copy(p, group_id(4, 0), 0, False))
        other_to_sib(ps, s - 1)

    def sib_wait(p, g):
        for other in (0, 1):
            sib_copy(p, g, other, True).wait_recv()

    def groups_at(s):
        return [g for g, (t, _) in enumerate(GROUPS) if t == s]

    def matmul_piece(p, g, at):
        m = p - 1
        zz = zpos(*GROUPS[g])
        if at == 0:
            sib_wait(p, g)
            for k in range(4):
                dist_copy(m, zz, k).wait()
        rows = pl.ds(pl.multiple_of(zz * (4 * R) + at * B, B), B)
        second[...] += jnp.dot(dist[m, :, rows], gbuf[m, rows, :], preferred_element_type=F32)

    def matmul(p, s):
        for g in groups_at(s):
            for at in range(4 * R // B):
                work.append(functools.partial(matmul_piece, p, g, at))

    def first_copy(m, n, at_col, dev, start, size):
        ref = fbuf.at[m, at_col, pl.ds(start, size)]
        n = m * 22 + n
        return remote(ref, ref, fs_sem.at[n], fr_sem.at[n], dev)

    def x_col(other, s, d):
        y = 1 - yhi if other else yhi
        return y * 4 + (x + 4 - d * s) % 4

    def way(d):
        return 0 if d == 1 else 1

    hi_col = (1 - yhi) * 4 + x

    def hi_copy(m, q, at_col):
        return first_copy(m, q, at_col, hi_dev, q * Q, Q)

    def own_copy(m, s, d, at_col):
        n = 4 + (s - 1) * 2 + way(d)
        if s == 1:
            return first_copy(m, n, at_col, x_dev[d], 0, R)
        return first_copy(m, n, at_col, x_dev[d], way(d) * 2 * Q, 2 * Q)

    def other_copy(m, q, s, d, at_col):
        n = 8 + q * 2 + way(d) if s == 1 else 16 + q
        return first_copy(m, n, at_col, x_dev[d], q * Q, Q)

    def hi_send(m, q):
        send(hi_copy(m, q, col))

    def own_send(m):
        for d in DIRS:
            send(own_copy(m, 1, d, col))

    def own_pass(m):
        for d in DIRS:
            own_copy(m, 1, d, x_col(0, 1, d)).wait_recv()
            send(own_copy(m, 2, d, x_col(0, 1, d)))

    def own_end(m):
        for d in DIRS:
            own_copy(m, 2, d, x_col(0, 2, d)).wait_recv()

    def hi_pass(m, q):
        hi_copy(m, q, hi_col).wait_recv()
        for d in DIRS:
            send(other_copy(m, q, 1, d, hi_col))

    def other_pass(m, q):
        for d in DIRS:
            other_copy(m, q, 1, d, x_col(1, 1, d)).wait_recv()
        d = 1 if q < 2 else -1
        send(other_copy(m, q, 2, d, x_col(1, 1, d)))

    def other_end(m):
        for q in range(4):
            d = 1 if q < 2 else -1
            other_copy(m, q, 2, d, x_col(1, 2, d)).wait_recv()

    def multiply(m, c):
        rows = pl.ds(pl.multiple_of(c * B, B), B)
        acc[m] += jnp.dot(fbuf[m, c], tbuf[rows, :], preferred_element_type=F32)

    def multiply_group(m, g):
        sib_wait(0, g)
        multiply(m, zpos(*GROUPS[g]))

    def keep(m):
        piece_rows = pl.ds(pl.multiple_of(row * R, R), R)
        gbuf[m, piece_rows, :] = acc[m].astype(BF16)

    def build_line(m, other, steps):
        base = (1 - yhi if other else yhi) * 4
        for k in steps:
            work.append(functools.partial(multiply, m, base + (x + k) % 4))

    def build_groups(m, s):
        for g in groups_at(s):
            work.append(functools.partial(multiply_group, m, g))

    def prepare_start():
        for copy in own_in[NP + 1 :]:
            copy.wait()
        stat[...] = to_sublanes(stype[...].reshape(1, B).astype(F32))

    def prepare(m, at):
        kinds = ttype[...].reshape(1, B).astype(F32)
        rows = pl.ds(m * R + at, RT)
        affinity = lax.dot_general(
            sfeat[rows, :], tfeat[...], (((1,), (1,)), ((), ())), preferred_element_type=F32
        )
        base = jnp.log(fbuf[m, col, pl.ds(at, RT), :].astype(F32))
        own = stat[rows, :]
        for k in range(B // 128):
            cut = slice(k * 128, (k + 1) * 128)
            mismatch = jnp.where(own != kinds[:, cut], 1.0, 0.0).astype(F32)
            pre[rows, cut] = (
                base[:, cut]
                + feature_weight / math.sqrt(FEAT) * affinity[:, cut]
                - mismatch_cost * mismatch
            )

    later = functools.partial
    td, g0, g1 = ((p,) for p in range(3))
    own_in[0].wait()
    own_in[NP].wait()
    phase_start(td, later(hi_send, 0, 0))
    hi_send(0, 1)
    own_send(0)
    for m in range(NP):
        for s, d in GROUPS:
            for k in range(4):
                dist_copy(m, zpos(s, d), k).start()
    for ref in (acc, second):
        ref[...] = jnp.zeros_like(ref)
    phase_other(td)
    hi_send(0, 2)
    hi_send(0, 3)
    own_in[1].wait()

    def nothing():
        pass

    work += [nothing, nothing, later(own_pass, 0), later(hi_pass, 0, 0), later(hi_pass, 0, 1)]
    phase_step(td, 1)
    do_all()
    work += [nothing, later(hi_pass, 0, 2), nothing, nothing, later(hi_pass, 0, 3)]
    phase_step(td, 2)
    do_all()
    hi_send(1, 0)
    work += [nothing, later(other_pass, 0, 0), later(other_pass, 0, 1), nothing, later(other_pass, 0, 2)]
    phase_step(td, 3)
    do_all()
    work += [nothing, later(other_pass, 0, 3)]
    phase_step(td, 4)
    hi_send(1, 1)
    own_send(1)
    other_to_sib(td, 4)
    own_end(0)
    other_end(0)
    for s in range(5):
        build_groups(0, s)
    work.append(later(keep, 0))
    do_all()
    phase_start(g0)
    prepare_start()
    for at in range(0, R, RT):
        work.append(later(prepare, 0, at))
    phase_other(g0)
    hi_send(1, 2)
    own_pass(1)
    hi_pass(1, 0)
    work.append(later(hi_pass, 1, 1))
    for at in range(0, R, RT):
        work.append(later(prepare, 1, at))
    phase_step(g0, 1)
    hi_send(1, 3)
    work.append(later(other_pass, 1, 0))
    work.append(later(hi_pass, 1, 2))
    work.append(later(own_end, 1))
    build_line(1, 0, range(4))
    phase_step(g0, 2, 2)
    work.append(later(other_pass, 1, 1))
    work.append(later(hi_pass, 1, 3))
    work.append(later(other_pass, 1, 2))
    build_line(1, 1, (0,))
    work.append(later(other_pass, 1, 3))
    build_line(1, 1, (1, 3))
    phase_step(g0, 3, 2)
    do_all()
    other_end(1)
    build_line(1, 1, (2,))
    work.append(later(keep, 1))
    do_all()
    phase_start(g1)
    matmul(1, 0)
    matmul(1, 1)
    phase_step(g0, 4)
    do_all()
    phase_other(g1)
    matmul(1, 2)
    work.insert(2, later(other_to_sib, g0, 4))
    phase_step(g1, 1)
    matmul(1, 3)
    matmul(1, 4)
    phase_step(g1, 2, 2)
    matmul(2, 0)
    phase_step(g1, 3, 2)
    matmul(2, 1)
    matmul(2, 2)
    phase_step(g1, 4, 2)
    matmul(2, 3)
    do_some(2)
    other_to_sib(g1, 4)
    matmul(2, 4)
    do_all()

    def row_steps(body):
        lax.fori_loop(0, B // RS, lambda i, _: (body(pl.ds(pl.multiple_of(i * RS, RS), RS)), 0)[1], 0)

    spot = lax.broadcasted_iota(jnp.int32, (RT, 128), 1)

    def row_stats(rows):
        score = pre[rows, :] + coupling_weight * second[rows, :]
        pre[rows, :] = score
        top = jnp.max(score, axis=1, keepdims=True)
        total = jnp.sum(jnp.exp(score - top), axis=1, keepdims=True)
        stat[rows, :] = jnp.where(
            lax.broadcasted_iota(jnp.int32, (RS, 128), 1) < 64, top, total
        )

    row_steps(row_stats)
    turned = jnp.transpose(stat[...])
    rstat[col] = lanes_to_tile(turned[0:1, :], turned[64:65, :])
    for j in range(1, NCOL):
        send(
            remote(
                rstat.at[col],
                rstat.at[col],
                rs_sem.at[j],
                rr_sem.at[j],
                (row, (col + j) % NCOL),
            )
        )
    for j in range(1, NCOL):
        came = (col + NCOL - j) % NCOL
        remote(rstat.at[came], rstat.at[came], rs_sem.at[j], rr_sem.at[j], (row, came)).wait_recv()

    def combined(ref):
        tops = ref[:, 0:4, :]
        top = jnp.max(tops, axis=0)
        total = jnp.sum(ref[:, 4:8, :] * jnp.exp(tops - top[None]), axis=0)
        return top + jnp.log(total)

    row_lse = tile_to_lanes(combined(rstat))
    shift = jnp.log(roww[...].reshape(1, B)) + math.log(NCOL * B) - row_lse
    stat[...] = to_sublanes(shift)

    def shifted(rows, best):
        move = stat[rows, :]
        tops = []
        for k in range(B // 128):
            cut = slice(k * 128, (k + 1) * 128)
            value = pre[rows, cut] + move
            pre[rows, cut] = value
            tops.append(jnp.max(value, axis=0, keepdims=True))
        return jnp.maximum(best, jnp.concatenate(tops, axis=1))

    def over_rows(body, start):
        return lax.fori_loop(
            0, B // RS, lambda i, c: body(pl.ds(pl.multiple_of(i * RS, RS), RS), c), start
        )

    col_top = over_rows(shifted, jnp.full((1, B), -jnp.inf, F32))
    col_sum = over_rows(
        lambda rows, c: c + jnp.sum(jnp.exp(pre[rows, :] - col_top), axis=0, keepdims=True),
        jnp.zeros((1, B), F32),
    )
    cstat[row] = lanes_to_tile(col_top, col_sum)
    for j in range(1, NROW):
        send(
            remote(
                cstat.at[row],
                cstat.at[row],
                cs_sem.at[j],
                cr_sem.at[j],
                ((row + j) % NROW, col),
            )
        )
    for j in range(1, NROW):
        came = (row + NROW - j) % NROW
        remote(cstat.at[came], cstat.at[came], cs_sem.at[j], cr_sem.at[j], (came, col)).wait_recv()
    col_shift = (
        jnp.log(colw[...].reshape(1, B)) + math.log(NROW * B) - tile_to_lanes(combined(cstat))
    )

    def part_of(c):
        return parts.at[pl.ds(pl.multiple_of(c * SB, SB), SB)]

    for j in (6, 2, 5, 7, 4, 3, 1, 0):
        goes = (col + j) % NCOL
        rows = pl.ds(pl.multiple_of(goes * SB, SB), SB)
        value = jnp.exp(pre[rows, :] + col_shift)
        rounded = value.astype(BF16)
        next_out[rows, :] = rounded
        parts[rows, 0:FEAT] = jnp.dot(rounded, tfeat[...], preferred_element_type=F32).astype(BF16)
        mass = jnp.sum(value, axis=1, keepdims=True)
        high = mass.astype(BF16).astype(F32)
        parts[rows, FEAT : FEAT + 128] = jnp.where(spot < 64, high, mass - high).astype(BF16)
        if j:
            send(remote(part_of(goes), got.at[col], ps_sem.at[j], pr_sem.at[j], (row, goes)))
    out_copy = pltpu.make_async_copy(next_out, next_hbm, out_sem.at[0])
    out_copy.start()

    total = parts[pl.ds(pl.multiple_of(col * SB, SB), SB), :].astype(F32)
    for j in range(1, NCOL):
        came = (col + NCOL - j) % NCOL
        remote(part_of(came), got.at[came], ps_sem.at[j], pr_sem.at[j], (row, came)).wait_recv()
        total = total + got[came].astype(F32)
    mass = total[:, FEAT : FEAT + 1] + total[:, FEAT + 64 : FEAT + 65]
    bary_out[...] = (total[:, 0:FEAT] / mass).astype(BF16)
    bary_copy = pltpu.make_async_copy(bary_out, bary_hbm, out_sem.at[1])
    bary_copy.start()

    for copy in started:
        copy.wait_send()
    out_copy.wait()
    bary_copy.wait()


def hand_over(next_in, bary_in, next_out, bary_out, sem):
    copies = (
        pltpu.make_async_copy(next_in, next_out, sem.at[0]),
        pltpu.make_async_copy(bary_in, bary_out, sem.at[1]),
    )
    for copy in copies:
        copy.start()
    for copy in copies:
        copy.wait()


def shards(*args):
    anywhere = pl.BlockSpec(memory_space=pl.ANY)
    dma = pltpu.SemaphoreType.DMA
    results = (
        pl.pallas_call(
            kernel,
            out_shape=(
                jax.ShapeDtypeStruct((B, B), BF16),
                jax.ShapeDtypeStruct((SB, FEAT), BF16),
            ),
            in_specs=[anywhere] * 9,
            out_specs=(anywhere, anywhere),
            scratch_shapes=[
                pltpu.VMEM((NP, B, NROW * R), BF16),
                pltpu.VMEM((NROW * TB, B), BF16),
                pltpu.VMEM((NP, NROW * R, B), BF16),
                pltpu.VMEM((NP, NCOL, R, B), BF16),
                pltpu.VMEM((NP, R, B), F32),
                pltpu.VMEM((B, B), F32),
                pltpu.VMEM((B, B), F32),
                pltpu.VMEM((B, FEAT), BF16),
                pltpu.VMEM((B, FEAT), BF16),
                pltpu.VMEM((B,), jnp.int32),
                pltpu.VMEM((B,), jnp.int32),
                pltpu.VMEM((B,), F32),
                pltpu.VMEM((B,), F32),
                pltpu.VMEM((B, 128), F32),
                pltpu.VMEM((NCOL, 8, 128), F32),
                pltpu.VMEM((NROW, 8, 128), F32),
                pltpu.VMEM((B, B), BF16),
                pltpu.VMEM((SB, FEAT), BF16),
                pltpu.VMEM((B, FEAT + 128), BF16),
                pltpu.VMEM((NCOL, SB, FEAT + 128), BF16),
                dma((NP + 7,)),
                dma((NP * NROW,)),
                dma((2,)),
                dma((72,)),
                dma((72,)),
                dma((27,)),
                dma((27,)),
                dma((48,)),
                dma((48,)),
                dma((44,)),
                dma((44,)),
                dma((NCOL,)),
                dma((NCOL,)),
                dma((NROW,)),
                dma((NROW,)),
                dma((NCOL,)),
                dma((NCOL,)),
            ],
            compiler_params=pltpu.CompilerParams(
                collective_id=0, has_side_effects=True, vmem_limit_bytes=60 * 2**20
            ),
            name="mirror_step",
        )(*args)
    )
    return tuple(
        pl.pallas_call(
            hand_over,
            out_shape=tuple(jax.ShapeDtypeStruct(r.shape, r.dtype) for r in results),
            in_specs=[pl.BlockSpec(memory_space=pltpu.VMEM)] * 2,
            out_specs=(anywhere, anywhere),
            scratch_shapes=[dma((2,))],
            name="hand_over",
        )(*results)
    )


def solution(mesh):
    in_specs = (
        P("row", "col"),
        P("row", None),
        P("row", "col"),
        P("row", None),
        P("col", None),
        P("row"),
        P("col"),
        P("row"),
        P("col"),
    )
    out_specs = (P("row", "col"), P(("row", "col"), None))
    return jax.shard_map(shards, mesh=mesh, in_specs=in_specs, out_specs=out_specs, check_vma=False)
```

```python
import functools
import math

import jax
import jax.numpy as jnp
from jax import lax
from jax.experimental import pallas as pl
from jax.experimental.pallas import tpu as pltpu
from jax.sharding import PartitionSpec as P

MESH = pl.DeviceIdType.MESH
F32 = jnp.float32
BF16 = jnp.bfloat16

coupling_weight = 0.5
feature_weight = 2.5
mismatch_cost = 1.0

NZ = 8
NROW = 32
NCOL = 8
B = 512
NP = 2
R = B // NP
Q = R // 4
TB = 128
SB = B // NCOL
FEAT = 256
RT = 64
RS = 128
DIRS = (1, -1)
GROUPS = [(0, 0)] + [(s, d) for s in (1, 2, 3) for d in DIRS] + [(4, 1)]


def group_id(s, d):
    return GROUPS.index((s, {0: 0, 4: 1}.get(s, d)))


def lanes_to_tile(top, bottom):
    return jnp.concatenate(
        [v[:, k * 128 : (k + 1) * 128] for v in (top, bottom) for k in range(B // 128)], axis=0
    )


def tile_to_lanes(tile):
    return jnp.concatenate([tile[k : k + 1, :] for k in range(B // 128)], axis=1)


def to_sublanes(row):
    return jnp.transpose(jnp.broadcast_to(row, (128, B)))


def kernel(
    coupling,
    source_dist,
    target_dist,
    source_feat,
    target_feat,
    source_type,
    target_type,
    row_weight,
    col_weight,
    next_hbm,
    bary_hbm,
    dist,
    tbuf,
    gbuf,
    fbuf,
    acc,
    second,
    pre,
    sfeat,
    tfeat,
    stype,
    ttype,
    roww,
    colw,
    stat,
    rstat,
    cstat,
    next_out,
    bary_out,
    parts,
    got,
    in_sem,
    dist_sem,
    out_sem,
    zs_sem,
    zr_sem,
    ys_sem,
    yr_sem,
    bs_sem,
    br_sem,
    fs_sem,
    fr_sem,
    rs_sem,
    rr_sem,
    cs_sem,
    cr_sem,
    ps_sem,
    pr_sem,
):
    row = lax.axis_index("row")
    col = lax.axis_index("col")
    z = row // 4
    lane = (row // 2) % 2
    core = row % 2
    x = col % 4
    yhi = col // 4

    def row_at(zz, line):
        return zz * 4 + line * 2 + core

    def zpos(s, d):
        return (z + NZ - d * s) % NZ

    z_dev = {d: (((z + NZ + d) % NZ) * 4 + lane * 2 + core, col) for d in DIRS}
    y_dev = (z * 4 + (1 - lane) * 2 + core, col)
    sib_dev = (z * 4 + lane * 2 + 1 - core, col)
    x_dev = {d: (row, yhi * 4 + (x + 4 + d) % 4) for d in DIRS}
    hi_dev = (row, (1 - yhi) * 4 + x)

    barrier = pltpu.get_barrier_semaphore()
    near = (*z_dev.values(), y_dev, sib_dev, *x_dev.values(), hi_dev)
    for dev in near:
        pl.semaphore_signal(barrier, inc=1, device_id=dev, device_id_type=MESH)
    own_in = []

    def bring(k, src, dst):
        copy = pltpu.make_async_copy(src, dst, in_sem.at[k])
        copy.start()
        own_in.append(copy)

    for m in range(NP):
        bring(m, coupling.at[pl.ds(m * R, R)], fbuf.at[m, col])
    own_rows = pl.ds(pl.multiple_of(row * TB, TB), TB)
    bring(NP, target_dist, tbuf.at[own_rows])
    bring(3, source_feat, sfeat)
    bring(4, target_feat, tfeat)
    bring(5, source_type, stype)
    bring(6, target_type, ttype)
    bring(7, row_weight, roww)
    bring(8, col_weight, colw)

    def dist_copy(m, zz, k):
        origin = zz * 4 + k
        src = pl.ds(pl.multiple_of(origin * B + m * R, R), R)
        dst = pl.ds(pl.multiple_of(origin * R, R), R)
        return pltpu.make_async_copy(
            source_dist.at[:, src], dist.at[m, :, dst], dist_sem.at[m * NROW + origin]
        )

    pl.semaphore_wait(barrier, len(near))

    started = []

    def remote(src, dst, ssem, rsem, dev):
        return pltpu.make_async_remote_copy(
            src_ref=src,
            dst_ref=dst,
            send_sem=ssem,
            recv_sem=rsem,
            device_id=dev,
            device_id_type=MESH,
        )

    def send(copy):
        copy.start()
        started.append(copy)

    bufs = [tbuf] + [gbuf.at[m] for m in range(NP)]
    sizes = [TB] + [R] * NP
    fronts = [TB // 4] + [R // 2] * NP

    def piece(p, origin, part, quarter=None):
        size = sizes[p] - fronts[p] if part else fronts[p]
        start = origin * sizes[p] + part * fronts[p]
        if quarter is not None:
            size //= 2
            start = start + quarter * size
        return bufs[p].at[pl.ds(pl.multiple_of(start, 16), size)]

    def whole(p, origin):
        return bufs[p].at[pl.ds(pl.multiple_of(origin * sizes[p], sizes[p]), sizes[p])]

    KIND = [(0, 0), (0, 1), (1, 1)]

    def z_copy(p, kind, s, d, origin_z):
        other, part = KIND[kind]
        line = 1 - lane if other else lane
        quarter = None if s < 4 else (0 if d == 1 else 1)
        ref = piece(p, row_at(origin_z, line), part, quarter)
        n = ((p * 3 + kind) * 2 + (0 if d == 1 else 1)) * 4 + s - 1
        return remote(ref, ref, zs_sem.at[n], zr_sem.at[n], z_dev[d])

    def y_send_copy(p, g, part, incoming):
        s, d = GROUPS[g]
        line = 1 - lane if incoming else lane
        ref = piece(p, row_at(zpos(s, d), line), part)
        n = p * 9 + (8 if part == 1 else g)
        return remote(ref, ref, ys_sem.at[n], yr_sem.at[n], y_dev)

    def sib_copy(p, g, other, incoming):
        s, d = GROUPS[g]
        line = 1 - lane if other else lane
        origin = zpos(s, d) * 4 + line * 2 + (1 - core if incoming else core)
        ref = whole(p, origin)
        n = (p * 8 + g) * 2 + other
        return remote(ref, ref, bs_sem.at[n], br_sem.at[n], sib_dev)

    def z_forward(p, kind, s, d):
        if s < 4:
            send(z_copy(p, kind, s + 1, d, zpos(s, d)))

    def phase_start(ps, then=lambda: None):
        for p in ps:
            send(y_send_copy(p, 0, 1, False))
        then()
        for kind in (0, 1):
            for p in ps:
                for d in DIRS:
                    send(z_copy(p, kind, 1, d, z))
        for p in ps:
            send(y_send_copy(p, 0, 0, False))
            send(sib_copy(p, 0, 0, False))

    def phase_other(ps):
        for p in ps:
            y_send_copy(p, 0, 1, True).wait_recv()
            for d in DIRS:
                send(z_copy(p, 2, 1, d, z))

    def other_to_sib(ps, s):
        for p in ps:
            for d in DIRS if s in (1, 2, 3) else (0,):
                g = group_id(s, d)
                y_send_copy(p, g, 0, True).wait_recv()
                send(sib_copy(p, g, 1, False))

    work = []

    def do_some(count=1):
        for _ in range(min(count, len(work))):
            work.pop(0)()

    def do_all():
        do_some(len(work))

    def phase_step(ps, s, count=1):
        for kind in (0, 1, 2):
            for p in ps:
                for d in DIRS:
                    z_copy(p, kind, s, d, zpos(s, d)).wait_recv()
                    z_forward(p, kind, s, d)
                    if kind == 0 and s < 4:
                        send(y_send_copy(p, group_id(s, d), 0, False))
                    if kind == 1 and s < 4:
                        send(sib_copy(p, group_id(s, d), 0, False))
                    do_some(count)
                if kind == 0 and s == 4:
                    send(y_send_copy(p, group_id(4, 0), 0, False))
                if kind == 1 and s == 4:
                    send(sib_copy(p, group_id(4, 0), 0, False))
        other_to_sib(ps, s - 1)

    def sib_wait(p, g):
        for other in (0, 1):
            sib_copy(p, g, other, True).wait_recv()

    def groups_at(s):
        return [g for g, (t, _) in enumerate(GROUPS) if t == s]

    def matmul_piece(p, g, at):
        m = p - 1
        zz = zpos(*GROUPS[g])
        if at == 0:
            sib_wait(p, g)
            for k in range(4):
                dist_copy(m, zz, k).wait()
        rows = pl.ds(pl.multiple_of(zz * (4 * R) + at * B, B), B)
        second[...] += jnp.dot(dist[m, :, rows], gbuf[m, rows, :], preferred_element_type=F32)

    def matmul(p, s):
        for g in groups_at(s):
            for at in range(4 * R // B):
                work.append(functools.partial(matmul_piece, p, g, at))

    def first_copy(m, n, at_col, dev, start, size):
        ref = fbuf.at[m, at_col, pl.ds(start, size)]
        n = m * 22 + n
        return remote(ref, ref, fs_sem.at[n], fr_sem.at[n], dev)

    def x_col(other, s, d):
        y = 1 - yhi if other else yhi
        return y * 4 + (x + 4 - d * s) % 4

    def way(d):
        return 0 if d == 1 else 1

    hi_col = (1 - yhi) * 4 + x

    def hi_copy(m, q, at_col):
        return first_copy(m, q, at_col, hi_dev, q * Q, Q)

    def own_copy(m, s, d, at_col):
        n = 4 + (s - 1) * 2 + way(d)
        if s == 1:
            return first_copy(m, n, at_col, x_dev[d], 0, R)
        return first_copy(m, n, at_col, x_dev[d], way(d) * 2 * Q, 2 * Q)

    def other_copy(m, q, s, d, at_col):
        n = 8 + q * 2 + way(d) if s == 1 else 16 + q
        return first_copy(m, n, at_col, x_dev[d], q * Q, Q)

    def hi_send(m, q):
        send(hi_copy(m, q, col))

    def own_send(m):
        for d in DIRS:
            send(own_copy(m, 1, d, col))

    def own_pass(m):
        for d in DIRS:
            own_copy(m, 1, d, x_col(0, 1, d)).wait_recv()
            send(own_copy(m, 2, d, x_col(0, 1, d)))

    def own_end(m):
        for d in DIRS:
            own_copy(m, 2, d, x_col(0, 2, d)).wait_recv()

    def hi_pass(m, q):
        hi_copy(m, q, hi_col).wait_recv()
        for d in DIRS:
            send(other_copy(m, q, 1, d, hi_col))

    def other_pass(m, q):
        for d in DIRS:
            other_copy(m, q, 1, d, x_col(1, 1, d)).wait_recv()
        d = 1 if q < 2 else -1
        send(other_copy(m, q, 2, d, x_col(1, 1, d)))

    def other_end(m):
        for q in range(4):
            d = 1 if q < 2 else -1
            other_copy(m, q, 2, d, x_col(1, 2, d)).wait_recv()

    def multiply(m, c):
        rows = pl.ds(pl.multiple_of(c * B, B), B)
        acc[m] += jnp.dot(fbuf[m, c], tbuf[rows, :], preferred_element_type=F32)

    def multiply_group(m, g):
        sib_wait(0, g)
        multiply(m, zpos(*GROUPS[g]))

    def keep(m):
        piece_rows = pl.ds(pl.multiple_of(row * R, R), R)
        gbuf[m, piece_rows, :] = acc[m].astype(BF16)

    def build_line(m, other, steps):
        base = (1 - yhi if other else yhi) * 4
        for k in steps:
            work.append(functools.partial(multiply, m, base + (x + k) % 4))

    def build_groups(m, s):
        for g in groups_at(s):
            work.append(functools.partial(multiply_group, m, g))

    def prepare_start():
        for copy in own_in[NP + 1 :]:
            copy.wait()
        stat[...] = to_sublanes(stype[...].reshape(1, B).astype(F32))

    def prepare(m, at):
        kinds = ttype[...].reshape(1, B).astype(F32)
        rows = pl.ds(m * R + at, RT)
        affinity = lax.dot_general(
            sfeat[rows, :], tfeat[...], (((1,), (1,)), ((), ())), preferred_element_type=F32
        )
        base = jnp.log(fbuf[m, col, pl.ds(at, RT), :].astype(F32))
        own = stat[rows, :]
        for k in range(B // 128):
            cut = slice(k * 128, (k + 1) * 128)
            mismatch = jnp.where(own != kinds[:, cut], 1.0, 0.0).astype(F32)
            pre[rows, cut] = (
                base[:, cut]
                + feature_weight / math.sqrt(FEAT) * affinity[:, cut]
                - mismatch_cost * mismatch
            )

    later = functools.partial
    td, g0, g1 = ((p,) for p in range(3))
    own_in[0].wait()
    own_in[NP].wait()
    phase_start(td, later(hi_send, 0, 0))
    hi_send(0, 1)
    own_send(0)
    for m in range(NP):
        for s, d in GROUPS:
            for k in range(4):
                dist_copy(m, zpos(s, d), k).start()
    for ref in (acc, second):
        ref[...] = jnp.zeros_like(ref)
    phase_other(td)
    hi_send(0, 2)
    hi_send(0, 3)
    own_in[1].wait()

    def nothing():
        pass

    work += [nothing, nothing, later(own_pass, 0), later(hi_pass, 0, 0), later(hi_pass, 0, 1)]
    phase_step(td, 1)
    do_all()
    work += [nothing, later(hi_pass, 0, 2), nothing, nothing, later(hi_pass, 0, 3)]
    phase_step(td, 2)
    do_all()
    hi_send(1, 0)
    work += [nothing, later(other_pass, 0, 0), later(other_pass, 0, 1), nothing, later(other_pass, 0, 2)]
    phase_step(td, 3)
    do_all()
    work += [nothing, later(other_pass, 0, 3)]
    phase_step(td, 4)
    hi_send(1, 1)
    own_send(1)
    other_to_sib(td, 4)
    own_end(0)
    other_end(0)
    for s in range(5):
        build_groups(0, s)
    work.append(later(keep, 0))
    do_all()
    phase_start(g0)
    hi_send(1, 2)
    prepare_start()
    for at in range(0, R, RT):
        work.append(later(prepare, 0, at))
    phase_other(g0)
    hi_send(1, 3)
    own_pass(1)
    hi_pass(1, 0)
    work.append(later(hi_pass, 1, 1))
    for at in range(0, R, RT):
        work.append(later(prepare, 1, at))
    phase_step(g0, 1)
    work.append(later(other_pass, 1, 0))
    work.append(later(hi_pass, 1, 2))
    work.append(later(own_end, 1))
    work.append(later(other_pass, 1, 1))
    work.append(later(hi_pass, 1, 3))
    build_line(1, 0, range(4))
    phase_step(g0, 2, 2)
    work.append(later(other_pass, 1, 2))
    build_line(1, 1, (0,))
    work.append(later(other_pass, 1, 3))
    build_line(1, 1, (1, 3))
    phase_step(g0, 3, 2)
    do_all()
    other_end(1)
    build_line(1, 1, (2,))
    work.append(later(keep, 1))
    do_all()
    phase_start(g1)
    matmul(1, 0)
    matmul(1, 1)
    phase_step(g0, 4)
    do_all()
    phase_other(g1)
    matmul(1, 2)
    work.insert(2, later(other_to_sib, g0, 4))
    phase_step(g1, 1)
    matmul(1, 3)
    matmul(1, 4)
    phase_step(g1, 2, 2)
    matmul(2, 0)
    phase_step(g1, 3, 2)
    matmul(2, 1)
    matmul(2, 2)
    phase_step(g1, 4, 2)
    matmul(2, 3)
    do_some(2)
    other_to_sib(g1, 4)
    matmul(2, 4)
    do_all()

    def row_steps(body):
        lax.fori_loop(0, B // RS, lambda i, _: (body(pl.ds(pl.multiple_of(i * RS, RS), RS)), 0)[1], 0)

    spot = lax.broadcasted_iota(jnp.int32, (RT, 128), 1)

    def row_stats(rows):
        score = pre[rows, :] + coupling_weight * second[rows, :]
        pre[rows, :] = score
        top = jnp.max(score, axis=1, keepdims=True)
        total = jnp.sum(jnp.exp(score - top), axis=1, keepdims=True)
        stat[rows, :] = jnp.where(
            lax.broadcasted_iota(jnp.int32, (RS, 128), 1) < 64, top, total
        )

    row_steps(row_stats)
    turned = jnp.transpose(stat[...])
    rstat[col] = lanes_to_tile(turned[0:1, :], turned[64:65, :])
    for j in range(1, NCOL):
        send(
            remote(
                rstat.at[col],
                rstat.at[col],
                rs_sem.at[j],
                rr_sem.at[j],
                (row, (col + j) % NCOL),
            )
        )
    for j in range(1, NCOL):
        came = (col + NCOL - j) % NCOL
        remote(rstat.at[came], rstat.at[came], rs_sem.at[j], rr_sem.at[j], (row, came)).wait_recv()

    def combined(ref):
        tops = ref[:, 0:4, :]
        top = jnp.max(tops, axis=0)
        total = jnp.sum(ref[:, 4:8, :] * jnp.exp(tops - top[None]), axis=0)
        return top + jnp.log(total)

    row_lse = tile_to_lanes(combined(rstat))
    shift = jnp.log(roww[...].reshape(1, B)) + math.log(NCOL * B) - row_lse
    stat[...] = to_sublanes(shift)

    def shifted(rows, best):
        move = stat[rows, :]
        tops = []
        for k in range(B // 128):
            cut = slice(k * 128, (k + 1) * 128)
            value = pre[rows, cut] + move
            pre[rows, cut] = value
            tops.append(jnp.max(value, axis=0, keepdims=True))
        return jnp.maximum(best, jnp.concatenate(tops, axis=1))

    def over_rows(body, start):
        return lax.fori_loop(
            0, B // RS, lambda i, c: body(pl.ds(pl.multiple_of(i * RS, RS), RS), c), start
        )

    col_top = over_rows(shifted, jnp.full((1, B), -jnp.inf, F32))
    col_sum = over_rows(
        lambda rows, c: c + jnp.sum(jnp.exp(pre[rows, :] - col_top), axis=0, keepdims=True),
        jnp.zeros((1, B), F32),
    )
    cstat[row] = lanes_to_tile(col_top, col_sum)
    for j in range(1, NROW):
        send(
            remote(
                cstat.at[row],
                cstat.at[row],
                cs_sem.at[j],
                cr_sem.at[j],
                ((row + j) % NROW, col),
            )
        )
    for j in range(1, NROW):
        came = (row + NROW - j) % NROW
        remote(cstat.at[came], cstat.at[came], cs_sem.at[j], cr_sem.at[j], (came, col)).wait_recv()
    col_shift = (
        jnp.log(colw[...].reshape(1, B)) + math.log(NROW * B) - tile_to_lanes(combined(cstat))
    )

    def part_of(c):
        return parts.at[pl.ds(pl.multiple_of(c * SB, SB), SB)]

    for j in (6, 2, 5, 7, 4, 3, 1, 0):
        goes = (col + j) % NCOL
        rows = pl.ds(pl.multiple_of(goes * SB, SB), SB)
        value = jnp.exp(pre[rows, :] + col_shift)
        rounded = value.astype(BF16)
        next_out[rows, :] = rounded
        parts[rows, 0:FEAT] = jnp.dot(rounded, tfeat[...], preferred_element_type=F32).astype(BF16)
        mass = jnp.sum(value, axis=1, keepdims=True)
        high = mass.astype(BF16).astype(F32)
        parts[rows, FEAT : FEAT + 128] = jnp.where(spot < 64, high, mass - high).astype(BF16)
        if j:
            send(remote(part_of(goes), got.at[col], ps_sem.at[j], pr_sem.at[j], (row, goes)))
    out_copy = pltpu.make_async_copy(next_out, next_hbm, out_sem.at[0])
    out_copy.start()

    total = parts[pl.ds(pl.multiple_of(col * SB, SB), SB), :].astype(F32)
    for j in range(1, NCOL):
        came = (col + NCOL - j) % NCOL
        remote(part_of(came), got.at[came], ps_sem.at[j], pr_sem.at[j], (row, came)).wait_recv()
        total = total + got[came].astype(F32)
    mass = total[:, FEAT : FEAT + 1] + total[:, FEAT + 64 : FEAT + 65]
    bary_out[...] = (total[:, 0:FEAT] / mass).astype(BF16)
    bary_copy = pltpu.make_async_copy(bary_out, bary_hbm, out_sem.at[1])
    bary_copy.start()

    for copy in started:
        copy.wait_send()
    out_copy.wait()
    bary_copy.wait()


def hand_over(next_in, bary_in, next_out, bary_out, sem):
    copies = (
        pltpu.make_async_copy(next_in, next_out, sem.at[0]),
        pltpu.make_async_copy(bary_in, bary_out, sem.at[1]),
    )
    for copy in copies:
        copy.start()
    for copy in copies:
        copy.wait()


def shards(*args):
    anywhere = pl.BlockSpec(memory_space=pl.ANY)
    dma = pltpu.SemaphoreType.DMA
    results = (
        pl.pallas_call(
            kernel,
            out_shape=(
                jax.ShapeDtypeStruct((B, B), BF16),
                jax.ShapeDtypeStruct((SB, FEAT), BF16),
            ),
            in_specs=[anywhere] * 9,
            out_specs=(anywhere, anywhere),
            scratch_shapes=[
                pltpu.VMEM((NP, B, NROW * R), BF16),
                pltpu.VMEM((NROW * TB, B), BF16),
                pltpu.VMEM((NP, NROW * R, B), BF16),
                pltpu.VMEM((NP, NCOL, R, B), BF16),
                pltpu.VMEM((NP, R, B), F32),
                pltpu.VMEM((B, B), F32),
                pltpu.VMEM((B, B), F32),
                pltpu.VMEM((B, FEAT), BF16),
                pltpu.VMEM((B, FEAT), BF16),
                pltpu.VMEM((B,), jnp.int32),
                pltpu.VMEM((B,), jnp.int32),
                pltpu.VMEM((B,), F32),
                pltpu.VMEM((B,), F32),
                pltpu.VMEM((B, 128), F32),
                pltpu.VMEM((NCOL, 8, 128), F32),
                pltpu.VMEM((NROW, 8, 128), F32),
                pltpu.VMEM((B, B), BF16),
                pltpu.VMEM((SB, FEAT), BF16),
                pltpu.VMEM((B, FEAT + 128), BF16),
                pltpu.VMEM((NCOL, SB, FEAT + 128), BF16),
                dma((NP + 7,)),
                dma((NP * NROW,)),
                dma((2,)),
                dma((72,)),
                dma((72,)),
                dma((27,)),
                dma((27,)),
                dma((48,)),
                dma((48,)),
                dma((44,)),
                dma((44,)),
                dma((NCOL,)),
                dma((NCOL,)),
                dma((NROW,)),
                dma((NROW,)),
                dma((NCOL,)),
                dma((NCOL,)),
            ],
            compiler_params=pltpu.CompilerParams(
                collective_id=0, has_side_effects=True, vmem_limit_bytes=60 * 2**20
            ),
            name="mirror_step",
        )(*args)
    )
    return tuple(
        pl.pallas_call(
            hand_over,
            out_shape=tuple(jax.ShapeDtypeStruct(r.shape, r.dtype) for r in results),
            in_specs=[pl.BlockSpec(memory_space=pltpu.VMEM)] * 2,
            out_specs=(anywhere, anywhere),
            scratch_shapes=[dma((2,))],
            name="hand_over",
        )(*results)
    )


def solution(mesh):
    in_specs = (
        P("row", "col"),
        P("row", None),
        P("row", "col"),
        P("row", None),
        P("col", None),
        P("row"),
        P("col"),
        P("row"),
        P("col"),
    )
    out_specs = (P("row", "col"), P(("row", "col"), None))
    return jax.shard_map(shards, mesh=mesh, in_specs=in_specs, out_specs=out_specs, check_vma=False)
```
